512 devices in a mesh: section: 8 (over z_lo), tensor: 16 (over z_hi, y, core), dp: 4 (over x).
Axes of the slice: x: 4, y: 4, z: 16 (z_hi: 2, z_lo: 8; z = z_hi * 8 + z_lo), core: 2. Of those that a mesh axis runs over, the one named last changes fastest.
Arguments:
- target_ids: int32 [4, 2048], P(None, 'section'), may hold values from 0 to 32127
- embed_table: bfloat16 [32128, 4096], P('dp', 'tensor'), may hold values from -16 to 16
- encoder_out: bfloat16 [4, 2048, 4096], P('dp', 'section', 'tensor'), may hold values from -32 to 32
- w_query: bfloat16 [4096, 4096], P(('section', 'dp'), 'tensor'), may hold values from -1 to 1
- w_key: bfloat16 [4096, 4096], P(('section', 'dp'), 'tensor'), may hold values from -1 to 1
- w_value: bfloat16 [4096, 4096], P(('section', 'dp'), 'tensor'), may hold values from -0.09375 to 0.09375
Outputs:
- attended: bfloat16 [4, 2048, 4096], P('dp', 'section', 'tensor')
The draws below stay inside these ranges and needn't reach their ends.
All inputs are finite; a program needn't handle non-finite values.
Results may differ from the reference program's by a relative error of at most 0.0096.
Values may be sent and summed in bfloat16 or wider, within the bound.
No kernel may reach another device: no remote copies, remote signals or barrier semaphores. Data moves between devices by JAX's collectives and lax.ppermute only.
A program may use at most 64 MiB of HBM per device.

```python
import math
import jax
import jax.numpy as jnp
from jax import lax

D = 4096
HEADS = 16
HD = 256
V = 32128
L = 2048
BATCH = 4


def query_matrix(key):
    normal_part = jnp.clip(jax.random.normal(jax.random.fold_in(key, 11), (D, HEADS * HD), jnp.float32), -6.0, 6.0)
    return 1.6 * normal_part / math.sqrt(D)


def draw_w_query(key, part):
    return jnp.clip(query_matrix(key), -1.0, 1.0).astype(jnp.bfloat16)


def draw_w_key(key, part):
    normal_part = jnp.clip(jax.random.normal(jax.random.fold_in(key, 12), (D, HEADS * HD), jnp.float32), -6.0, 6.0)
    other = 1.6 * normal_part / math.sqrt(D)
    result = other
    return jnp.clip(result, -1.0, 1.0).astype(jnp.bfloat16)


def draw_embed_table(key, part):
    normal_part = jnp.clip(jax.random.normal(jax.random.fold_in(key, 1), (V, D), jnp.float32), -6.0, 6.0)
    result = normal_part
    return jnp.clip(result, -16.0, 16.0).astype(jnp.bfloat16)


def draw_encoder_out(key, part):
    normal_part = jnp.clip(jax.random.normal(jax.random.fold_in(key, 3), (BATCH, L, D), jnp.float32), -6.0, 6.0)
    result = normal_part
    return jnp.clip(result, -32.0, 32.0).astype(jnp.bfloat16)


def touch_ends(entries, own_key, smallest, high):
    index_at = [jax.random.randint(jax.random.fold_in(own_key, axis), (), 0, length) for axis, length in enumerate(entries.shape)]
    widest = entries.shape.index(max(entries.shape))
    next_to = index_at[:widest] + [(index_at[widest] + 1) % entries.shape[widest]] + index_at[widest + 1:]
    return entries.at[tuple(index_at)].set(smallest).at[tuple(next_to)].set(high)


def steps_of(own_key, shape, cuts, low, largest):
    def one(position, blocks):
        draws = jax.random.uniform(jax.random.fold_in(jax.random.fold_in(own_key, 6), position), (blocks,), jnp.float32, low / len(cuts), largest / len(cuts))
        return jnp.repeat(jnp.exp(draws), shape[position] // blocks).reshape((-1,) + (1,) * (len(shape) - position - 1))

    gain = one(*cuts[0])
    for cut in cuts[1:]:
        gain = gain * one(*cut)
    return gain


def centred(stream_key, shape, deviation, limit, pieces=(), kind=jnp.bfloat16):
    factor_of = steps_of(stream_key, shape, pieces, -0.22, 0.18) if pieces else 1.0
    array = jax.random.normal(stream_key, shape, jnp.float32) * deviation * factor_of
    return jnp.minimum(jnp.maximum(array, -limit), limit).astype(kind)


def setup_inputs(seed: int = 0) -> dict:
    splits = jax.random.split(jax.random.key(seed), 7)
    return {
        "target_ids": touch_ends(jax.random.randint(splits[0], (BATCH, L), 0, V), jax.random.fold_in(splits[0], 1), 0, V - 1).astype(jnp.int32),
        "embed_table": draw_embed_table(jax.random.fold_in(splits[6], 71), 0),
        "encoder_out": draw_encoder_out(jax.random.fold_in(splits[6], 71), 0),
        "w_query": draw_w_query(jax.random.fold_in(splits[6], 71), 0),
        "w_key": draw_w_key(jax.random.fold_in(splits[6], 71), 0),
        "w_value": centred(splits[5], (D, HEADS * HD), D ** -0.5, 0.09375, ((0, 32), (1, 16))),
    }


def reference(target_ids, embed_table, encoder_out, w_query, w_key, w_value):
    decoder_in = jnp.take(embed_table, target_ids, axis=0)
    queries = jnp.dot(decoder_in.reshape(-1, D), w_query, preferred_element_type=jnp.float32).astype(jnp.bfloat16)
    memory = encoder_out.reshape(-1, D)
    keys = jnp.dot(memory, w_key, preferred_element_type=jnp.float32).astype(jnp.bfloat16)
    values = jnp.dot(memory, w_value, preferred_element_type=jnp.float32).astype(jnp.bfloat16)
    queries = queries.reshape(BATCH, L, HEADS, HD)
    keys = keys.reshape(BATCH, L, HEADS, HD)
    values = values.reshape(BATCH, L, HEADS, HD)
    logit_scale_factor = HD ** -0.5

    def one_head(head_index):
        head_query_slice = lax.dynamic_index_in_dim(queries, head_index, 2, keepdims=False).astype(jnp.float32)
        head_key_slice = lax.dynamic_index_in_dim(keys, head_index, 2, keepdims=False).astype(jnp.float32)
        head_value_slice = lax.dynamic_index_in_dim(values, head_index, 2, keepdims=False).astype(jnp.float32)
        attention_logits = jnp.einsum("trw,tew->tre", head_query_slice, head_key_slice) * logit_scale_factor
        peaks = jnp.max(attention_logits, axis=-1, keepdims=True)
        weights = jnp.exp(attention_logits - peaks)
        weight_sum = jnp.sum(weights, axis=-1, keepdims=True)
        reduced_precision_weights = lax.optimization_barrier(weights.astype(jnp.bfloat16)).astype(jnp.float32)
        weighted_value_total = jnp.einsum("onh,ohf->onf", reduced_precision_weights, head_value_slice, precision=lax.Precision.HIGHEST)
        return (weighted_value_total / weight_sum).astype(jnp.bfloat16)

    heads_out = lax.map(one_head, jnp.arange(HEADS, dtype=jnp.int32))
    return jnp.transpose(heads_out, (1, 2, 0, 3)).reshape(BATCH, L, HEADS * HD)
```

```python
import jax
import jax.numpy as jnp
from jax import lax
from jax.sharding import Mesh, PartitionSpec as P

HD = 256
F32 = jnp.float32
BF16 = jnp.bfloat16
AXES = ("zb", "q", "zhi", "y", "core", "dp")
SIZES = (4, 2, 2, 4, 2, 4)
SWAP = [(0, 1), (1, 0)]
NEAR = [(i, i ^ 1) for i in range(4)]
FAR = [(i, 3 - i) for i in range(4)]


def pair_gather(x, axis):
    half = x.shape[0] // 2
    a, b = x[:half], x[half:]
    a1 = lax.ppermute(a, axis, NEAR)
    b1 = lax.ppermute(b, axis, FAR)
    a = jnp.concatenate([a, a1])
    b = jnp.concatenate([b, b1])
    a2 = lax.ppermute(a, axis, FAR)
    b2 = lax.ppermute(b, axis, NEAR)
    return a, a2, b, b2


def on_device(target_ids, embed_table, encoder_out, w_query, w_key, w_value):
    core = lax.axis_index("core")
    x = lax.axis_index("dp")
    weights = jnp.concatenate([w_key, w_value, w_query], axis=1)
    weights = lax.all_gather(weights, ("zb", "q"), axis=0, tiled=True)
    rows = embed_table.shape[0]
    offset = target_ids - x * rows
    inside = (offset >= 0) & (offset < rows)
    picked = jnp.take(embed_table, jnp.clip(offset, 0, rows - 1), axis=0)
    picked = jnp.where(inside[..., None], picked, jnp.zeros_like(picked))
    both = jnp.concatenate([encoder_out, picked], axis=0)
    n, pos, feat = both.shape
    half = pos // 2
    mine = lax.dynamic_slice_in_dim(both, core * half, half, 1)
    other = lax.dynamic_slice_in_dim(both, (1 - core) * half, half, 1)
    got = lax.ppermute(other, "core", SWAP)
    first = jnp.where(core == 0, mine, got)
    second = jnp.where(core == 0, got, mine)
    fb = feat // 2
    chunks = jnp.stack(
        [first[..., :fb], first[..., fb:], second[..., :fb], second[..., fb:]]
    )
    parts = lax.all_to_all(chunks, "dp", 0, 0, tiled=True)
    enc = parts[:, 0]
    dec = jnp.sum(parts[:, 1:].astype(F32), axis=0).astype(BF16)
    ed = jnp.stack([enc, dec], axis=1)
    sent = jnp.stack([ed[j ^ (2 * h)] for j in range(4) for h in range(2)])
    rowed = lax.all_to_all(sent, ("zb", "zhi"), 0, 0, tiled=True)
    wide = lax.all_gather(rowed, "y", axis=0)
    far = lax.ppermute(wide, "core", SWAP)
    lo = jnp.where(core == 0, wide, far)
    hi = jnp.where(core == 0, far, wide)
    full = jnp.stack([lo, hi])
    full = full.reshape(2, 4, 4, 2, 2, half, fb)
    full = jnp.transpose(full, (4, 2, 0, 5, 3, 1, 6)).reshape(2, 4 * pos, 8 * fb)
    kv = jnp.dot(full[0], weights[:, : 2 * HD], preferred_element_type=F32)
    qq = jnp.dot(full[1], weights[:, 2 * HD :], preferred_element_type=F32)
    partial = jnp.concatenate([kv, qq], axis=1).reshape(4, pos, 3 * HD)
    sums = lax.all_to_all(partial, "dp", 0, 0, tiled=True)
    kvq = jnp.sum(sums, axis=0).astype(BF16)
    kv, queries = kvq[:, : 2 * HD], kvq[:, 2 * HD :]
    near = lax.ppermute(kv, "q", SWAP)
    kv = jnp.concatenate([kv, near])
    kv = jnp.concatenate(pair_gather(kv, "dp"))
    keys, values = kv[:, :HD], kv[:, HD:]
    logits = (
        lax.dot_general(queries, keys, (((1,), (1,)), ((), ())), preferred_element_type=F32)
        * HD ** (-0.5)
    )
    peak = jnp.max(logits, axis=-1, keepdims=True)
    w = jnp.exp(logits - peak)
    total = jnp.sum(w, axis=-1, keepdims=True)
    out = jnp.dot(w.astype(BF16), values, preferred_element_type=F32) / total
    out = out.astype(BF16)
    back = [
        (zb * 8 + h * 4 + xx, xx * 8 + h * 4 + (zb ^ (2 * h)))
        for zb in range(4)
        for h in range(2)
        for xx in range(4)
    ]
    out = lax.ppermute(out, ("zb", "zhi", "dp"), back)
    return out[None]


def solution(mesh):
    fine = Mesh(mesh.devices.reshape(SIZES), AXES)
    sec, ten = ("zb", "q"), ("zhi", "y", "core")
    in_specs = (
        P(None, sec),
        P("dp", ten),
        P("dp", sec, ten),
        P((*sec, "dp"), ten),
        P((*sec, "dp"), ten),
        P((*sec, "dp"), ten),
    )
    return jax.shard_map(
        on_device, mesh=fine, in_specs=in_specs, out_specs=P("dp", sec, ten), check_vma=False
    )
```

```python
import jax
import jax.numpy as jnp
from jax import lax
from jax.experimental import pallas as pl
from jax.experimental.pallas import tpu as pltpu
from jax.sharding import Mesh, PartitionSpec as P


HD = 256
F32 = jnp.float32
BF16 = jnp.bfloat16
AXES = ("zb", "q", "zhi", "y", "core", "dp")
SIZES = (4, 2, 2, 4, 2, 4)
SWAP = [(0, 1), (1, 0)]
NEAR = [(i, i ^ 1) for i in range(4)]
FAR = [(i, 3 - i) for i in range(4)]
ACROSS = [(i, i ^ 2) for i in range(4)]
W_ORDER = (0, 4, 2, 6, 1, 5, 3, 7)
TARGETS = (0, 1, 3, 2)
SMEM = pl.BlockSpec(memory_space=pltpu.SMEM)
VMEM = pl.BlockSpec(memory_space=pltpu.VMEM)


def project_kernel(order_ref, ids_ref, own_ref, far_ref, wa_ref, wb_ref, *out_refs, cols):
    core, me = ids_ref[0], ids_ref[1]
    rows, depth = own_ref.shape[1], wa_ref.shape[0]
    mine = pl.ds(pl.multiple_of(core * rows, rows), rows)
    other = pl.ds(pl.multiple_of((1 - core) * rows, rows), rows)
    apart = len(out_refs) > 1
    for i, target in enumerate(TARGETS):
        block = me ^ target if apart else i
        out_ref = out_refs[i] if apart else out_refs[0].at[i]

        def wide(ref):
            return jnp.concatenate([ref[order_ref[k] + block] for k in range(8)], axis=1)

        x = jnp.concatenate([wide(own_ref), wide(far_ref)], axis=0)
        res = jnp.dot(x[:, :depth], wa_ref[:, cols], preferred_element_type=F32)
        res += jnp.dot(x[:, depth:], wb_ref[:, cols], preferred_element_type=F32)
        if out_ref.dtype == BF16:
            keys = res[:, :HD]
            high = keys.astype(BF16)
            low = (keys - high.astype(F32)).astype(BF16)
            res = jnp.concatenate([high, low, res[:, HD:].astype(BF16)], axis=1)
        out_ref[mine, :] = res[:rows]
        out_ref[other, :] = res[rows:]


def project(order, ids, own, far, w, cols, apart):
    rows, n = own.shape[1], cols.stop - cols.start
    if apart:
        sent = jax.ShapeDtypeStruct((2 * rows, n + HD), BF16)
        out_shape = [jax.ShapeDtypeStruct((2 * rows, n), F32)] + [sent] * 3
    else:
        out_shape = jax.ShapeDtypeStruct((4, 2 * rows, n), F32)
    return pl.pallas_call(
        lambda *refs: project_kernel(*refs, cols=cols),
        out_shape=out_shape,
        in_specs=[SMEM, SMEM, VMEM, VMEM, VMEM, VMEM],
        out_specs=[VMEM] * 4 if apart else VMEM,
        cost_estimate=pl.CostEstimate(
            flops=32 * rows * w[0].shape[0] * n, bytes_accessed=8 << 20, transcendentals=0
        ),
    )(order, ids, own, far, *w)


def combine_kernel(own_ref, *refs):
    got_refs, out_ref = refs[:-1], refs[-1]
    keys, values = own_ref[:, :HD], own_ref[:, HD:]
    for ref in got_refs:
        keys += ref[:, :HD].astype(F32) + ref[:, HD : 2 * HD].astype(F32)
        values += ref[:, 2 * HD :].astype(F32)
    out_ref[:, :HD] = keys.astype(BF16)
    out_ref[:, HD:] = values.astype(BF16)


def attend_kernel(q_ref, *refs):
    kv_refs, out_ref, logits_ref = refs[:-2], refs[-2], refs[-1]
    q = q_ref[...]
    start, peak = 0, None
    for ref in kv_refs:
        n = ref.shape[0]
        s = lax.dot_general(
            q, ref[:, :HD], (((1,), (1,)), ((), ())), preferred_element_type=F32
        ) * HD ** (-0.5)
        logits_ref[:, start : start + n] = s
        top = jnp.max(s, axis=1, keepdims=True)
        peak = top if peak is None else jnp.maximum(peak, top)
        start += n
    start, total, acc = 0, 0.0, 0.0
    for ref in kv_refs:
        n = ref.shape[0]
        p = jnp.exp(logits_ref[:, start : start + n] - peak)
        total += jnp.sum(p, axis=1, keepdims=True)
        acc += jnp.dot(p.astype(BF16), ref[:, HD:], preferred_element_type=F32)
        start += n
    out_ref[...] = (acc / total).astype(BF16)


def attend(q, pieces):
    n = sum(p.shape[0] for p in pieces)
    return pl.pallas_call(
        attend_kernel,
        out_shape=jax.ShapeDtypeStruct(q.shape, BF16),
        in_specs=[VMEM] * (1 + len(pieces)),
        out_specs=VMEM,
        scratch_shapes=[pltpu.VMEM((q.shape[0], n), F32)],
        cost_estimate=pl.CostEstimate(
            flops=4 * q.shape[0] * n * HD, bytes_accessed=3 << 20, transcendentals=q.shape[0] * n
        ),
    )(q, *pieces)


def on_device(target_ids, embed_table, encoder_out, w_query, w_key, w_value):
    core = lax.axis_index("core")
    x = lax.axis_index("dp")
    z = lax.axis_index("zb") * 2 + lax.axis_index("q")
    section = z ^ jnp.array(W_ORDER, jnp.int32)
    order = (section & 3) * 8 + (section >> 2) * 4
    ids = jnp.stack([core, x]).astype(jnp.int32)
    pos, feat = encoder_out.shape[1:]
    half, fb = pos // 2, feat // 2

    def swap(value, axis):
        return lax.all_to_all(value, axis, 0, 0, tiled=True)

    def by_x(both):
        mine = lax.dynamic_slice_in_dim(both, core * half, half, 1)
        other = lax.dynamic_slice_in_dim(both, (1 - core) * half, half, 1)
        got = lax.ppermute(other, "core", SWAP)
        first = jnp.where(core == 0, mine, got)
        second = jnp.where(core == 0, got, mine)
        return jnp.stack(
            [first[..., :fb], first[..., fb:], second[..., :fb], second[..., fb:]]
        )

    def to_row(act):
        return swap(jnp.concatenate([act, act[2:], act[:2]]), ("zhi", "zb"))

    def over_y(act):
        got = swap(jnp.broadcast_to(act, (4, *act.shape)), "y")
        return got.reshape(32, half, fb)

    def gather_w(w):
        w1 = lax.ppermute(w, "zb", ACROSS)
        w = jnp.concatenate([w, w1])
        w2 = lax.ppermute(w, "zb", NEAR)
        w = jnp.concatenate([w, w2])
        return w, lax.ppermute(w, "q", SWAP)

    enc = swap(by_x(encoder_out), "dp")[:, 0]
    w = gather_w(jnp.concatenate([w_key, w_value, w_query], axis=1))
    rows = embed_table.shape[0]
    offset = target_ids - x * rows
    inside = (offset >= 0) & (offset < rows)
    picked = jnp.take(embed_table, jnp.clip(offset, 0, rows - 1), axis=0)
    picked = jnp.where(inside[..., None], picked, jnp.zeros_like(picked))
    enc = to_row(enc)
    enc, order, ids = lax.optimization_barrier((enc, order, ids))
    enc = over_y(enc)
    parts = by_x(picked)
    own, *sent = [lax.dynamic_index_in_dim(parts, x ^ t, 0, keepdims=False) for t in TARGETS]
    dec = own.astype(F32)
    for part, pairs in zip(sent, (NEAR, FAR, ACROSS)):
        dec += lax.ppermute(part, "dp", pairs).astype(F32)
    dec = dec.astype(BF16)
    dec = over_y(to_row(dec))
    enc_far = lax.ppermute(enc, "core", SWAP)
    dec_far = lax.ppermute(dec, "core", SWAP)

    def share(parts):
        got = [
            lax.ppermute(part, "dp", pairs)
            for part, pairs in zip(parts[1:], (NEAR, FAR, ACROSS))
        ]
        return pl.pallas_call(
            combine_kernel,
            out_shape=jax.ShapeDtypeStruct(parts[0].shape, BF16),
            in_specs=[VMEM] * 4,
            out_specs=VMEM,
            name="combine",
        )(parts[0], *got)

    parts = project(order, ids, enc, enc_far, w, slice(0, 2 * HD), True)
    kv = share(parts)
    parts = project(order, ids, dec, dec_far, w, slice(2 * HD, 3 * HD), False)
    queries = jnp.sum(swap(parts, "dp"), axis=0).astype(BF16)
    near = lax.ppermute(kv, "q", SWAP)
    a1 = lax.ppermute(kv, "dp", NEAR)
    b1 = lax.ppermute(near, "dp", FAR)
    a2 = lax.ppermute(jnp.concatenate([kv, a1]), "dp", FAR)
    b2 = lax.ppermute(jnp.concatenate([near, b1]), "dp", NEAR)
    out = attend(queries, (kv, near, a1, b1, a2, b2))
    back = [
        (zb * 8 + h * 4 + xx, xx * 8 + h * 4 + (zb ^ (2 * h)))
        for zb in range(4)
        for h in range(2)
        for xx in range(4)
    ]
    return lax.ppermute(out, ("zb", "zhi", "dp"), back)[None]


def solution(mesh):
    fine = Mesh(mesh.devices.reshape(SIZES), AXES)
    sec, ten = ("zb", "q"), ("zhi", "y", "core")
    in_specs = (
        P(None, sec),
        P("dp", ten),
        P("dp", sec, ten),
        P((*sec, "dp"), ten),
        P((*sec, "dp"), ten),
        P((*sec, "dp"), ten),
    )
    return jax.shard_map(
        on_device, mesh=fine, in_specs=in_specs, out_specs=P("dp", sec, ten), check_vma=False
    )
```
